128 devices in a mesh: tok: 32 (over y, x, core), head: 4 (over z).
Axes of the slice: x: 4, y: 4, z: 4, core: 2. Of those that a mesh axis runs over, the one named last changes fastest.
Arguments:
- queries: bfloat16 [32, 32768, 128], P('head', 'tok'), may hold values from -6 to 6
- keys: bfloat16 [4, 32768, 128], P('head', 'tok'), may hold values from -6 to 6
- values: bfloat16 [4, 32768, 128], P('head', 'tok'), may hold values from -6 to 6
- doc_lengths: int32 [16], replicated, may hold values from 1 to 8192, as said below
- tasks: int32 [512, 5], replicated, may hold values from 0 to 64, as said below
- w_out: bfloat16 [4096, 2048], P('head'), may hold values from -0.09375 to 0.09375
Outputs:
- projected: bfloat16 [32768, 2048], P('tok', 'head')
The draws below stay inside these ranges and needn't reach their ends.
Inputs may be any that keep to these rules, and one draw needn't show every extreme that they name: `doc_lengths`: the documents lie end to end; their lengths sum to 32768, and one is exactly 8192 tokens long. `tasks`: row t = qb * 8 + j describes query block qb (tokens qb * 512 to qb * 512 + 511) and head j of every group: column 0 is qb, column 1 is j, column 2 is the block that holds the first token of the document of the block's first token, column 3 is qb + 1, column 4 is the server, a token shard. Rows of one token shard's blocks name one server at most 1 times, 1 is reached, and every server is named in exactly 16 rows.
All inputs are finite; a program needn't handle non-finite values.
Results may differ from the reference program's by a relative error of at most 0.012.
Values may be sent and summed in bfloat16 or wider, within the bound.
A program may use at most 128 MiB of HBM per device.

```python
import jax
import jax.numpy as jnp
from jax import lax

D = 2048
QH = 32
KVH = 4
HD = 128
QBLK = 512
HG = 8
TOKENS = 32768
BLK_DEV = 2
QB = 64
DOC_MOST = 8192
NDOC = 16
N_TOK = 32


def documents(key):
    seeded = jax.random.fold_in(key, 101)
    weights = jax.random.randint(jax.random.fold_in(seeded, 1), (NDOC,), 32, 64, dtype=jnp.int32)
    longest = jax.random.randint(jax.random.fold_in(seeded, 2), (), 0, NDOC, dtype=jnp.int32)
    doc_index = jnp.arange(NDOC, dtype=jnp.int32)
    is_longest = doc_index == longest
    weights = jnp.where(is_longest, 0, weights)
    spare = TOKENS - DOC_MOST - (NDOC - 1)
    shares = spare * weights // jnp.sum(weights)
    leftover = spare - jnp.sum(shares)
    target = jnp.where(longest == 0, 1, 0)
    shares = shares + jnp.where(doc_index == target, leftover, 0)
    return jnp.where(is_longest, DOC_MOST, shares + 1).astype(jnp.int32)


def draw_doc_lengths(key, part):
    return documents(key)


def draw_tasks(key, part):
    lengths = documents(key)
    starts = jnp.cumsum(lengths) - lengths
    block_ids = jnp.arange(QB, dtype=jnp.int32)
    first_rows = block_ids * QBLK
    doc_begin = jnp.max(jnp.where(starts[None, :] <= first_rows[:, None], starts[None, :], 0), axis=1)
    low_block = doc_begin // QBLK
    high_block = block_ids + 1
    device_cost = jnp.sum((high_block - low_block).reshape(N_TOK, BLK_DEV), axis=1)
    device_ids = jnp.arange(N_TOK, dtype=jnp.int32)
    ordering = jnp.argsort(-(device_cost * N_TOK + (N_TOK - 1 - device_ids)))
    ranking = jnp.zeros((N_TOK,), jnp.int32).at[ordering].set(device_ids)
    spread = 2 * ranking % N_TOK + 2 * ranking // N_TOK
    heads = jnp.arange(HG, dtype=jnp.int32)
    owner = block_ids // BLK_DEV
    within = block_ids % BLK_DEV
    unit_slot = heads[None, :] * BLK_DEV + within[:, None]
    server = (spread[owner][:, None] + unit_slot) % N_TOK
    columns = [jnp.broadcast_to(block_ids[:, None], (QB, HG)), jnp.broadcast_to(heads[None, :], (QB, HG)), jnp.broadcast_to(low_block[:, None], (QB, HG)), jnp.broadcast_to(high_block[:, None], (QB, HG)), server]
    return jnp.stack(columns, axis=-1).reshape(QB * HG, 5).astype(jnp.int32)


def draw_queries(key, part):
    drawn = jnp.clip(jax.random.normal(jax.random.fold_in(key, 1), (QH, TOKENS, HD), jnp.float32), -6.0, 6.0)
    return drawn.astype(jnp.bfloat16)


def draw_keys(key, part):
    drawn = jnp.clip(jax.random.normal(jax.random.fold_in(key, 3), (KVH, TOKENS, HD), jnp.float32), -6.0, 6.0)
    return drawn.astype(jnp.bfloat16)


def level_of(key, dims, pieces, least, largest):
    factor_of = 1.0
    for axis_at, parts in pieces:
        draws = jax.random.uniform(jax.random.fold_in(jax.random.fold_in(key, 6), axis_at), (parts,), jnp.float32, least / len(pieces), largest / len(pieces))
        factor_of = factor_of * jnp.repeat(jnp.exp(draws), dims[axis_at] // parts).reshape((-1,) + (1,) * (len(dims) - 1 - axis_at))
    return factor_of


def centred(key, dims, scale, bound, shards=(), held_as=jnp.bfloat16):
    loudness = level_of(key, dims, shards, -0.22, 0.18) if shards else 1.0
    drawn = jax.random.normal(key, dims, jnp.float32) * scale * loudness
    return jnp.minimum(jnp.maximum(drawn, -bound), bound).astype(held_as)


def setup_inputs(seed: int = 0) -> dict:
    streams_of = jax.random.split(jax.random.key(seed), 7)
    queries = draw_queries(jax.random.fold_in(streams_of[6], 71), 0)
    keys = draw_keys(jax.random.fold_in(streams_of[6], 71), 0)
    values = centred(streams_of[2], (KVH, TOKENS, HD), 1.0, 6.0, ((0, 4), (1, 32)))
    doc_lengths = draw_doc_lengths(jax.random.fold_in(streams_of[6], 71), 0)
    tasks = draw_tasks(jax.random.fold_in(streams_of[6], 71), 0)
    w_out = centred(streams_of[5], (QH * HD, D), (QH * HD) ** -0.5, 0.09375, ((0, 4),))
    return dict(queries=queries, keys=keys, values=values, doc_lengths=doc_lengths, tasks=tasks, w_out=w_out)


FLOOR_SCORE = -1e30


def reference(queries, keys, values, doc_lengths, tasks, w_out):
    starts = jnp.cumsum(doc_lengths) - doc_lengths
    scaling = 1.0 / (HD ** 0.5)
    stride = 2 * QBLK
    offsets = jnp.arange(stride, dtype=jnp.int32)
    head_rows = jnp.arange(HG, dtype=jnp.int32)

    def one_block(block_id):
        positions = block_id * QBLK + jnp.arange(QBLK, dtype=jnp.int32)
        doc_begin = jnp.max(jnp.where(starts[None, :] <= positions[:, None], starts[None, :], 0), axis=1)
        task_rows = block_id * HG + head_rows
        low_keys = tasks[task_rows, 2] * QBLK
        high_keys = tasks[task_rows, 3] * QBLK
        query_block = lax.dynamic_slice_in_dim(queries, (block_id * QBLK).astype(jnp.int32), QBLK, 1)
        query_block = query_block.astype(jnp.float32).reshape(KVH, HG, QBLK, HD)
        first_key = jnp.min(low_keys)
        last_key = jnp.max(high_keys)
        turn_count = (last_key - first_key + stride - 1) // stride

        def window(step_index):
            key_start = first_key + step_index * stride
            window_start = jnp.clip(key_start, 0, TOKENS - stride).astype(jnp.int32)
            key_block = lax.dynamic_slice_in_dim(keys, window_start, stride, 1).astype(jnp.float32)
            value_block = lax.dynamic_slice_in_dim(values, window_start, stride, 1).astype(jnp.float32)
            key_pos = window_start + offsets
            scores = jnp.einsum("ghqe,gke->ghqk", query_block, key_block) * scaling
            inside = (key_pos >= key_start) & (key_pos < key_start + stride)
            visible = inside[None, None, :] & (key_pos[None, None, :] >= low_keys[:, None, None])
            visible = visible & (key_pos[None, None, :] < high_keys[:, None, None])
            visible = visible & (key_pos[None, None, :] >= doc_begin[None, :, None])
            visible = visible & (key_pos[None, None, :] <= positions[None, :, None])
            return scores, visible[None], value_block

        def find_peak(step_index, running):
            scores, visible, unused = window(step_index)
            return jnp.maximum(running, jnp.max(jnp.where(visible, scores, FLOOR_SCORE), axis=-1))

        row_peak = lax.fori_loop(0, turn_count, find_peak, jnp.full((KVH, HG, QBLK), FLOOR_SCORE, jnp.float32))

        def add_window(step_index, carried):
            row_total, weighted = carried
            scores, visible, value_block = window(step_index)
            expo = jnp.where(visible, jnp.exp(scores - row_peak[..., None]), 0.0)
            row_total = row_total + jnp.sum(expo, axis=-1)
            rounded = lax.optimization_barrier(expo.astype(jnp.bfloat16)).astype(jnp.float32)
            weighted = weighted + jnp.einsum("ghqk,gke->ghqe", rounded, value_block)
            return row_total, weighted

        initial = (jnp.zeros((KVH, HG, QBLK), jnp.float32), jnp.zeros((KVH, HG, QBLK, HD), jnp.float32))
        row_total, weighted = lax.fori_loop(0, turn_count, add_window, initial)
        attended = (weighted / row_total[..., None]).astype(jnp.bfloat16)
        return attended.reshape(QH, QBLK, HD)

    blocks = lax.map(one_block, jnp.arange(QB, dtype=jnp.int32))
    attended = blocks.transpose(0, 2, 1, 3).reshape(TOKENS, QH * HD)
    return jnp.dot(attended, w_out, preferred_element_type=jnp.float32).astype(jnp.bfloat16)
```

```python
import functools
import math

import jax
import jax.numpy as jnp
from jax import lax
from jax.experimental import pallas as pl
from jax.experimental.pallas import tpu as pltpu
from jax.sharding import PartitionSpec as P

MESH = pl.DeviceIdType.MESH
SHARD = 1024
HD = 128
BACK = 4
NWIN = 2 * BACK + 2
TQ = 256
TK = 1024
SUB = 256
HB = 4
QBLK = 512
NDOC = 16
SCALE = 1.0 / math.sqrt(HD)
LOG2E = math.log2(math.e)
C = SCALE * LOG2E
FLOOR = -1e30
LEAST = 2.0**-60
MOST = 2.0**100


def fetch_kernel(nchip, q_ref, kv_ref, qo_ref, win_ref, lsem, ssem, rsem, fs, fr, qs, qr):
    t = lax.axis_index("tok")
    c = t // 2
    k = lax.rem(t, 2)
    partner = t + 1 - 2 * k
    bar = pltpu.get_barrier_semaphore()
    peers = [partner]
    for d in range(1, BACK + 1):
        peers += [lax.rem(c + d, nchip) * 2 + k, lax.rem(c + nchip - d, nchip) * 2 + k]
    for p in peers:
        pl.semaphore_signal(bar, inc=1, device_id={"tok": p}, device_id_type=MESH)
    pl.semaphore_wait(bar, len(peers))

    def send(src, dst, s, r, tok):
        copy = pltpu.make_async_remote_copy(
            src_ref=src, dst_ref=dst, send_sem=s, recv_sem=r, device_id={"tok": tok}, device_id_type=MESH
        )
        copy.start()
        return copy

    own = pltpu.make_async_copy(kv_ref, win_ref.at[2 * BACK + k], lsem)
    own.start()
    sends = []
    for d in range(1, BACK + 1):
        sends.append(
            send(kv_ref, win_ref.at[2 * (BACK - d) + k], ssem.at[d], rsem.at[d], lax.rem(c + d, nchip) * 2 + k)
        )
    swap = send(kv_ref, win_ref.at[2 * BACK + k], ssem.at[0], rsem.at[0], partner)
    qswap = send(q_ref.at[pl.ds((1 - k) * HB, HB)], qo_ref, qs, qr, partner)
    onward = []
    for d in range(1, BACK + 1):
        sends[d - 1].wait_recv()
        slot = win_ref.at[2 * (BACK - d) + k]
        onward.append(send(slot, slot, fs.at[d], fr.at[d], partner))
    own.wait()
    swap.wait()
    qswap.wait()
    for s in sends:
        s.wait_send()
    for f in onward:
        f.wait()


def fetch(q, kv, nchip):
    return pl.pallas_call(
        functools.partial(fetch_kernel, nchip),
        in_specs=[pl.BlockSpec(memory_space=pl.ANY), pl.BlockSpec(memory_space=pltpu.VMEM)],
        out_specs=[pl.BlockSpec(memory_space=pl.ANY)] * 2,
        out_shape=[
            jax.ShapeDtypeStruct((HB, SHARD, HD), jnp.bfloat16),
            jax.ShapeDtypeStruct((NWIN, 2, SHARD, HD), jnp.bfloat16),
        ],
        scratch_shapes=[pltpu.SemaphoreType.DMA]
        + [pltpu.SemaphoreType.DMA((BACK + 1,))] * 4
        + [pltpu.SemaphoreType.DMA] * 2,
        compiler_params=pltpu.CompilerParams(collective_id=0, has_side_effects=True),
        name="fetch",
    )(q, kv)


def attend_kernel(
    n, doc_ref, lim_ref, q_ref, qf_ref, win_ref, o_ref, qbuf, kbuf, vbuf, acc, mrow, lrow, ready, qsem, wsem
):
    t = lax.axis_index("tok")
    k = lax.rem(t, 2)
    base = (t // 2 - BACK) * (2 * SHARD)

    qa = pltpu.make_async_copy(q_ref.at[pl.ds(k * HB, HB), pl.ds(n * TQ, TQ)], qbuf.at[0], qsem.at[0])
    qb = pltpu.make_async_copy(qf_ref.at[:, pl.ds(n * TQ, TQ)], qbuf.at[1], qsem.at[1])
    qa.start()
    qb.start()

    def tile_place(i):
        core = jnp.where(i == 0, k, 1 - k)
        p0 = (2 * BACK + core) * SHARD + n * TQ
        blk = (p0 + base) // QBLK
        low = lim_ref[2 * blk] * QBLK - base
        high = lim_ref[2 * blk + 1] * QBLK - base
        first = jnp.int32(-(2**30))
        last = jnp.int32(-(2**30))
        start = -base
        for d in range(NDOC):
            first = jnp.where(start <= p0, start, first)
            last = jnp.where(start <= p0 + TQ - 1, start, last)
            start = start + doc_ref[d]
        first = jnp.maximum(first, low)
        last = jnp.maximum(last, low)
        return p0, low, high, first, last

    def copies(j):
        return (
            pltpu.make_async_copy(win_ref.at[j, 0], kbuf.at[j], wsem.at[0, j]),
            pltpu.make_async_copy(win_ref.at[j, 1], vbuf.at[j, :, pl.ds(0, HD)], wsem.at[1, j]),
        )

    p00, _, _, f0, _ = tile_place(0)
    p01, _, _, f1, _ = tile_place(1)
    j_lo = jnp.clip(jnp.minimum(f0, f1) // SHARD, 0, NWIN - 1)
    j_hi = jnp.maximum(p00, p01) // SHARD + 1

    def begin(j, _):
        for cp in copies(j):
            cp.start()
        ready[j] = 0
        return 0

    lax.fori_loop(j_lo, j_hi, begin, 0)

    def need(j):
        @pl.when(ready[j] == 0)
        def _():
            for cp in copies(j):
                cp.wait()
            ready[j] = 1

    vbuf[:, :, HD:] = jnp.ones((NWIN, SHARD, HD), jnp.bfloat16)
    qa.wait()
    qb.wait()

    def tile(i, _):
        p0, low, high, first, last = tile_place(i)
        row = p0 + lax.broadcasted_iota(jnp.int32, (TQ, HD), 0)
        begins = jnp.full((TQ, HD), -(2**30), jnp.int32)
        start = -base
        for d in range(NDOC):
            begins = jnp.where(row >= start, start, begins)
            start = start + doc_ref[d]
        begins = jnp.maximum(begins, low)
        ends = jnp.minimum(row, high - 1)
        begins = jnp.concatenate([begins] * (SUB // HD), axis=1)
        ends = jnp.concatenate([ends] * (SUB // HD), axis=1)
        a0 = jnp.maximum(first, 0) // SUB
        a1 = (p0 + TQ) // SUB
        b0 = (jnp.maximum(last, 0) + TK - 1) // TK
        b1 = jnp.minimum(p0 + 1, high) // TK
        whole = b1 > b0
        na = jnp.where(whole, TK // SUB * b0, a1) - a0
        after = jnp.where(whole, TK // SUB * b1, a1)
        nm = na + a1 - after

        def sub_at(x):
            return jnp.where(x < na, a0 + x, after + x - na)

        def masked_scores(h, j, off, seen):
            kb = kbuf[j, pl.ds(off, SUB), :]
            s = lax.dot_general(qbuf[i, h], kb, (((1,), (1,)), ((), ())), preferred_element_type=jnp.float32) * C
            return jnp.where(seen, s, FLOOR)

        def seen_at(sub):
            pos = sub * SUB + lax.broadcasted_iota(jnp.int32, (TQ, SUB), 1)
            return (pos >= begins) & (pos <= ends)

        acc[...] = jnp.zeros(acc.shape, jnp.float32)

        def masked(x, _):
            sub = sub_at(x)
            j = sub // (SHARD // SUB)
            off = pl.multiple_of(lax.rem(sub, SHARD // SUB) * SUB, SUB)
            need(j)
            seen = seen_at(sub)
            vb = vbuf[j, pl.ds(off, SUB), :]
            for h in range(HB):
                p = jnp.exp2(masked_scores(h, j, off, seen))
                acc[h] += jnp.dot(p.astype(jnp.bfloat16), vb, preferred_element_type=jnp.float32)
            return 0

        def unmasked(j, _):
            need(j)
            kb = kbuf[j]
            vb = vbuf[j]
            for h in range(HB):
                s = lax.dot_general(qbuf[i, h], kb, (((1,), (1,)), ((), ())), preferred_element_type=jnp.float32) * C
                p = jnp.exp2(s).astype(jnp.bfloat16)
                acc[h] += jnp.dot(p, vb, preferred_element_type=jnp.float32)
            return 0

        lax.fori_loop(0, nm, masked, 0)
        lax.fori_loop(b0, jnp.where(whole, b1, b0), unmasked, 0)

        smallest = jnp.float32(MOST)
        largest = jnp.float32(LEAST)
        for h in range(HB):
            total = acc[h][:, HD:]
            smallest = jnp.minimum(smallest, jnp.min(total))
            largest = jnp.maximum(largest, jnp.max(total))
        fits = (smallest >= LEAST) & (largest <= MOST)

        @pl.when(fits)
        def _():
            for h in range(HB):
                whole_acc = acc[h]
                o_ref[i, h] = (whole_acc[:, :HD] / whole_acc[:, HD:]).astype(jnp.bfloat16)

        @pl.when(jnp.logical_not(fits))
        def _():
            def one_head(h, _):
                mrow[...] = jnp.full(mrow.shape, FLOOR, jnp.float32)
                lrow[...] = jnp.zeros(lrow.shape, jnp.float32)
                acc[0] = jnp.zeros(acc.shape[1:], jnp.float32)

                def step(sub, _):
                    j = sub // (SHARD // SUB)
                    off = pl.multiple_of(lax.rem(sub, SHARD // SUB) * SUB, SUB)
                    need(j)
                    seen = seen_at(sub)
                    s = masked_scores(h, j, off, seen)
                    old = mrow[...]
                    new = jnp.maximum(old, jnp.max(s, axis=1, keepdims=True))
                    p = jnp.where(seen, jnp.exp2(s - new[:, :1]), 0.0)
                    keep = jnp.exp2(old - new)
                    mrow[...] = new
                    lrow[...] = lrow[...] * keep + jnp.sum(p, axis=1, keepdims=True)
                    vb = vbuf[j, pl.ds(off, SUB), pl.ds(0, HD)]
                    acc[0, :, pl.ds(0, HD)] = acc[0, :, pl.ds(0, HD)] * keep + jnp.dot(
                        p.astype(jnp.bfloat16), vb, preferred_element_type=jnp.float32
                    )
                    return 0

                lax.fori_loop(a0, a1, step, 0)
                o_ref[i, h] = (acc[0, :, pl.ds(0, HD)] / lrow[...]).astype(jnp.bfloat16)
                return 0

            lax.fori_loop(0, HB, one_head, 0)

        return 0

    lax.fori_loop(0, 2, tile, 0)

    def finish(j, _):
        need(j)
        return 0

    lax.fori_loop(j_lo, j_hi, finish, 0)


def attend(n, q, qf, win, doc_lengths, limits):
    smem = pl.BlockSpec(memory_space=pltpu.SMEM)
    hbm = pl.BlockSpec(memory_space=pl.ANY)
    return pl.pallas_call(
        functools.partial(attend_kernel, n),
        in_specs=[smem, smem, hbm, hbm, hbm],
        out_specs=pl.BlockSpec(memory_space=pltpu.VMEM),
        out_shape=jax.ShapeDtypeStruct((2, HB, TQ, HD), jnp.bfloat16),
        scratch_shapes=[
            pltpu.VMEM((2, HB, TQ, HD), jnp.bfloat16),
            pltpu.VMEM((NWIN, SHARD, HD), jnp.bfloat16),
            pltpu.VMEM((NWIN, SHARD, 2 * HD), jnp.bfloat16),
            pltpu.VMEM((HB, TQ, 2 * HD), jnp.float32),
            pltpu.VMEM((TQ, HD), jnp.float32),
            pltpu.VMEM((TQ, HD), jnp.float32),
            pltpu.SMEM((NWIN,), jnp.int32),
            pltpu.SemaphoreType.DMA((2,)),
            pltpu.SemaphoreType.DMA((2, NWIN)),
        ],
        compiler_params=pltpu.CompilerParams(vmem_limit_bytes=40 * 2**20),
        cost_estimate=pl.CostEstimate(flops=8 * 10**9, bytes_accessed=6 * 2**20, transcendentals=16 * 10**6),
        name="attend",
    )(doc_lengths, limits, q, qf, win)


def local(queries, keys, values, doc_lengths, tasks, w_out):
    n_tok = lax.axis_size("tok")
    n_head = lax.axis_size("head")
    t = lax.axis_index("tok")
    z = lax.axis_index("head")
    core = lax.rem(t, 2)
    width = w_out.shape[1] // n_head
    limits = tasks.reshape(-1, 8, 5)[:, 0, 2:4].reshape(-1)
    kv = jnp.concatenate([keys, values], axis=0)
    qf, win = fetch(queries, kv, n_tok // 2)
    swap = [(i, i ^ 1) for i in range(n_tok)]
    weights = w_out.reshape(2 * HB, HD, -1)
    pieces = []
    for n in range(SHARD // TQ):
        out = attend(n, queries, qf, win, doc_lengths, limits)
        back = lax.ppermute(out[1], "tok", swap)
        lower = jnp.where(core == 0, out[0], back)
        upper = jnp.where(core == 0, back, out[0])
        part = jnp.einsum(
            "hte,hed->td",
            jnp.concatenate([lower, upper], axis=0),
            weights,
            preferred_element_type=jnp.float32,
        ).astype(jnp.bfloat16)
        total = lax.dynamic_slice_in_dim(part, z * width, width, 1).astype(jnp.float32)
        for d in range(1, n_head):
            block = lax.dynamic_slice_in_dim(part, lax.rem(z + d, n_head) * width, width, 1)
            got = lax.ppermute(block, "head", [(i, (i + d) % n_head) for i in range(n_head)])
            total = total + got.astype(jnp.float32)
        pieces.append(total.astype(jnp.bfloat16))
    return jnp.concatenate(pieces, axis=0)


def solution(mesh):
    in_specs = (
        P("head", "tok", None),
        P("head", "tok", None),
        P("head", "tok", None),
        P(),
        P(),
        P("head", None),
    )
    return jax.shard_map(local, mesh=mesh, in_specs=in_specs, out_specs=P("tok", "head"), check_vma=False)
```

```python
import functools
import math

import jax
import jax.numpy as jnp
from jax import lax
from jax.experimental import pallas as pl
from jax.experimental.pallas import tpu as pltpu
from jax.sharding import PartitionSpec as P


MESH = pl.DeviceIdType.MESH
SHARD = 1024
HD = 128
BACK = 4
NWIN = 2 * BACK + 2
TQ = 256
TK = 1024
SUB = 256
HB = 4
QBLK = 512
NDOC = 16
CALLS = (
    ((1, 0), (1, 1)),
    ((0, 0), (1, 2)),
    ((0, 1), (1, 3)),
    ((0, 2),),
    ((0, 3),),
)
SCALE = 1.0 / math.sqrt(HD)
LOG2E = math.log2(math.e)
C = SCALE * LOG2E
FLOOR = -1e30
LEAST = 2.0**-60
MOST = 2.0**100


def fetch_kernel(ny, nx, q_ref, k_ref, v_ref, qo_ref, win_ref, relay, own_sem, send_sem, recv_sem, fwd_sem, got_sem, swap_sem):
    t = lax.axis_index("tok")
    chip = t // 2
    k = lax.rem(t, 2)
    y = chip // nx
    x = lax.rem(chip, nx)

    def at(row, col):
        return (row * nx + col) * 2 + k

    partner = t + 1 - 2 * k
    down = at(lax.rem(y + 1, ny), x)
    up = at(lax.rem(y + ny - 1, ny), x)
    right = at(y, lax.rem(x + 1, nx))
    left = at(y, lax.rem(x + nx - 1, nx))
    bar = pltpu.get_barrier_semaphore()
    peers = (partner, down, up, right, left)
    for p in peers:
        pl.semaphore_signal(bar, inc=1, device_id={"tok": p}, device_id_type=MESH)
    pl.semaphore_wait(bar, len(peers))

    def remote(src, dst, s, r, tok):
        return pltpu.make_async_remote_copy(
            src_ref=src, dst_ref=dst, send_sem=s, recv_sem=r, device_id={"tok": tok}, device_id_type=MESH
        )

    mine = (k_ref.at[0], v_ref.at[0])

    def slot(d, m):
        return win_ref.at[2 * (BACK - d) + k, m]

    above = [remote(mine[m], slot(BACK, m), send_sem.at[BACK, m], recv_sem.at[BACK, m], down) for m in range(2)]
    for cp in above:
        cp.start()

    def across(d, m, src):
        dst = slot(d, m)
        to = right if d == 1 else left
        if d == 2:
            dst = relay.at[m]
            to = right if m == 0 else left
        return remote(src, dst, send_sem.at[d, m], recv_sem.at[0, m] if d == 2 else recv_sem.at[d, m], to)

    order = (1, 3, 2)
    for m in range(2):
        for d in order:

            @pl.when(x + d < nx)
            def _():
                across(d, m, mine[m]).start()

    keep = [pltpu.make_async_copy(mine[m], slot(0, m), own_sem.at[m]) for m in range(2)]
    for cp in keep:
        cp.start()
    swaps = [remote(mine[m], slot(0, m), fwd_sem.at[0, m], got_sem.at[0, m], partner) for m in range(2)]
    for cp in swaps:
        cp.start()
    qswap = remote(q_ref.at[pl.ds((1 - k) * HB, HB)], qo_ref, swap_sem.at[0], swap_sem.at[1], partner)
    qswap.start()

    onward = []

    def pass_on(d, m):
        cp = remote(slot(d, m), slot(d, m), fwd_sem.at[d, m], got_sem.at[d, m], partner)
        cp.start()
        onward.append(cp)

    for m in range(2):
        above[m].wait_recv()
        for d in order:

            @pl.when(x + d >= nx)
            def _():
                across(d, m, slot(BACK, m)).start()

        pass_on(BACK, m)

    hops = []
    for m in range(2):
        across(2, m, mine[m]).wait_recv()
        hop = remote(relay.at[m], slot(2, m), send_sem.at[0, m], recv_sem.at[2, m], right if m == 0 else left)
        hop.start()
        hops.append(hop)
        for d in (1, 3):
            across(d, m, mine[m]).wait_recv()
            pass_on(d, m)
    for m in range(2):
        hops[m].wait_recv()
        pass_on(2, m)

    for m in range(2):
        keep[m].wait()
        above[m].wait_send()
        swaps[m].wait()
        hops[m].wait_send()
        for d in order:
            across(d, m, mine[m]).wait_send()
    qswap.wait()
    for cp in onward:
        cp.wait()


def fetch(q, keys, values, ny, nx):
    vmem = pl.BlockSpec(memory_space=pltpu.VMEM)
    hbm = pl.BlockSpec(memory_space=pl.ANY)
    return pl.pallas_call(
        functools.partial(fetch_kernel, ny, nx),
        in_specs=[hbm, vmem, vmem],
        out_specs=[hbm] * 2,
        out_shape=[
            jax.ShapeDtypeStruct((HB, SHARD, HD), jnp.bfloat16),
            jax.ShapeDtypeStruct((NWIN, 2, SHARD, HD), jnp.bfloat16),
        ],
        scratch_shapes=[
            pltpu.VMEM((2, SHARD, HD), jnp.bfloat16),
            pltpu.SemaphoreType.DMA((2,)),
            pltpu.SemaphoreType.DMA((BACK + 1, 2)),
            pltpu.SemaphoreType.DMA((BACK + 1, 2)),
            pltpu.SemaphoreType.DMA((BACK + 1, 2)),
            pltpu.SemaphoreType.DMA((BACK + 1, 2)),
            pltpu.SemaphoreType.DMA((2,)),
        ],
        compiler_params=pltpu.CompilerParams(collective_id=0, has_side_effects=True),
        name="fetch",
    )(q, keys, values)


def attend_kernel(
    tiles, doc_ref, lim_ref, q_ref, qf_ref, win_ref, o_ref, qbuf, kbuf, vbuf, acc, mrow, lrow, ready, qsem, wsem
):
    t = lax.axis_index("tok")
    k = lax.rem(t, 2)
    base = (t // 2 - BACK) * (2 * SHARD)

    loads = []
    for i, (side, r) in enumerate(tiles):
        src = qf_ref if side else q_ref.at[pl.ds(k * HB, HB)]
        loads.append(pltpu.make_async_copy(src.at[:, pl.ds(r * TQ, TQ)], qbuf.at[i], qsem.at[i]))
        loads[i].start()

    def tile_place(i):
        core, r = k, tiles[0][1]
        if tiles[0][0]:
            core = 1 - k
        for m in range(1, len(tiles)):
            core = jnp.where(i == m, 1 - k if tiles[m][0] else k, core)
            r = jnp.where(i == m, tiles[m][1], r)
        p0 = (2 * BACK + core) * SHARD + r * TQ
        blk = (p0 + base) // QBLK
        low = lim_ref[2 * blk] * QBLK - base
        high = lim_ref[2 * blk + 1] * QBLK - base
        first = jnp.int32(-(2**30))
        last = jnp.int32(-(2**30))
        start = -base
        for d in range(NDOC):
            first = jnp.where(start <= p0, start, first)
            last = jnp.where(start <= p0 + TQ - 1, start, last)
            start = start + doc_ref[d]
        first = jnp.maximum(first, low)
        last = jnp.maximum(last, low)
        return p0, low, high, first, last

    def copies(j):
        return (
            pltpu.make_async_copy(win_ref.at[j, 0], kbuf.at[j], wsem.at[0, j]),
            pltpu.make_async_copy(win_ref.at[j, 1], vbuf.at[j, :, pl.ds(0, HD)], wsem.at[1, j]),
        )

    j_lo = jnp.int32(NWIN - 1)
    for m in range(len(tiles)):
        j_lo = jnp.minimum(j_lo, jnp.maximum(tile_place(jnp.int32(m))[3], 0) // SHARD)
    j_hi = jnp.int32(NWIN)

    def begin(j, _):
        for cp in copies(j):
            cp.start()
        ready[j] = 0
        return 0

    lax.fori_loop(j_lo, j_hi, begin, 0)

    def need(j):
        @pl.when(ready[j] == 0)
        def _():
            for cp in copies(j):
                cp.wait()
            ready[j] = 1

    vbuf[:, :, HD:] = jnp.ones((NWIN, SHARD, HD), jnp.bfloat16)
    for load in loads:
        load.wait()

    def tile(i, _):
        p0, low, high, first, last = tile_place(i)
        row = p0 + lax.broadcasted_iota(jnp.int32, (TQ, HD), 0)
        begins = jnp.full((TQ, HD), -(2**30), jnp.int32)
        start = -base
        for d in range(NDOC):
            begins = jnp.where(row >= start, start, begins)
            start = start + doc_ref[d]
        begins = jnp.maximum(begins, low)
        ends = jnp.minimum(row, high - 1)
        old = begins <= first
        begins = jnp.concatenate([begins] * (SUB // HD), axis=1)
        ends = jnp.concatenate([ends] * (SUB // HD), axis=1)
        a0 = jnp.maximum(first, 0) // SUB
        a1 = (p0 + TQ) // SUB
        b0 = (jnp.maximum(first, 0) + TK - 1) // TK
        b1 = jnp.minimum(p0 + 1, high) // TK
        whole = b1 > b0
        na = jnp.where(whole, TK // SUB * b0, a1) - a0
        after = jnp.where(whole, TK // SUB * b1, a1)
        nm = na + a1 - after

        def sub_at(x):
            return jnp.where(x < na, a0 + x, after + x - na)

        def masked_scores(h, j, off, seen):
            kb = kbuf[j, pl.ds(off, SUB), :]
            s = lax.dot_general(qbuf[i, h], kb, (((1,), (1,)), ((), ())), preferred_element_type=jnp.float32) * C
            return jnp.where(seen, s, FLOOR)

        def seen_at(sub):
            pos = sub * SUB + lax.broadcasted_iota(jnp.int32, (TQ, SUB), 1)
            return (pos >= begins) & (pos <= ends)

        acc[...] = jnp.zeros(acc.shape, jnp.float32)

        def masked(x, _):
            sub = sub_at(x)
            j = sub // (SHARD // SUB)
            off = pl.multiple_of(lax.rem(sub, SHARD // SUB) * SUB, SUB)
            need(j)
            seen = seen_at(sub)
            vb = vbuf[j, pl.ds(off, SUB), :]
            for h in range(HB):
                p = jnp.exp2(masked_scores(h, j, off, seen))
                acc[h] += jnp.dot(p.astype(jnp.bfloat16), vb, preferred_element_type=jnp.float32)
            return 0

        def unmasked(j, _):
            need(j)
            kb = kbuf[j]
            vb = vbuf[j]
            for h in range(HB):
                s = lax.dot_general(qbuf[i, h], kb, (((1,), (1,)), ((), ())), preferred_element_type=jnp.float32) * C
                p = jnp.exp2(s).astype(jnp.bfloat16)
                acc[h] += jnp.dot(p, vb, preferred_element_type=jnp.float32)
            return 0

        lax.fori_loop(b0, jnp.where(whole, b1, b0), unmasked, 0)

        @pl.when(last > first)
        def _():
            for h in range(HB):
                for w in range(2):
                    cols = pl.ds(w * HD, HD)
                    acc[h, :, cols] = jnp.where(old, acc[h, :, cols], 0.0)

        lax.fori_loop(0, nm, masked, 0)

        smallest = jnp.float32(MOST)
        largest = jnp.float32(LEAST)
        for h in range(HB):
            total = acc[h][:, HD:]
            smallest = jnp.minimum(smallest, jnp.min(total))
            largest = jnp.maximum(largest, jnp.max(total))
        fits = (smallest >= LEAST) & (largest <= MOST)

        @pl.when(fits)
        def _():
            for h in range(HB):
                whole_acc = acc[h]
                o_ref[i, h] = (whole_acc[:, :HD] / whole_acc[:, HD:]).astype(jnp.bfloat16)

        @pl.when(jnp.logical_not(fits))
        def _():
            def one_head(h, _):
                mrow[...] = jnp.full(mrow.shape, FLOOR, jnp.float32)
                lrow[...] = jnp.zeros(lrow.shape, jnp.float32)
                acc[0] = jnp.zeros(acc.shape[1:], jnp.float32)

                def step(sub, _):
                    j = sub // (SHARD // SUB)
                    off = pl.multiple_of(lax.rem(sub, SHARD // SUB) * SUB, SUB)
                    need(j)
                    seen = seen_at(sub)
                    s = masked_scores(h, j, off, seen)
                    old = mrow[...]
                    new = jnp.maximum(old, jnp.max(s, axis=1, keepdims=True))
                    p = jnp.where(seen, jnp.exp2(s - new[:, :1]), 0.0)
                    keep = jnp.exp2(old - new)
                    mrow[...] = new
                    lrow[...] = lrow[...] * keep + jnp.sum(p, axis=1, keepdims=True)
                    vb = vbuf[j, pl.ds(off, SUB), pl.ds(0, HD)]
                    acc[0, :, pl.ds(0, HD)] = acc[0, :, pl.ds(0, HD)] * keep + jnp.dot(
                        p.astype(jnp.bfloat16), vb, preferred_element_type=jnp.float32
                    )
                    return 0

                lax.fori_loop(a0, a1, step, 0)
                o_ref[i, h] = (acc[0, :, pl.ds(0, HD)] / lrow[...]).astype(jnp.bfloat16)
                return 0

            lax.fori_loop(0, HB, one_head, 0)

        return 0

    lax.fori_loop(0, len(tiles), tile, 0)

    def finish(j, _):
        need(j)
        return 0

    lax.fori_loop(j_lo, j_hi, finish, 0)


def attend(tiles, q, qf, win, doc_lengths, limits):
    smem = pl.BlockSpec(memory_space=pltpu.SMEM)
    hbm = pl.BlockSpec(memory_space=pl.ANY)
    return pl.pallas_call(
        functools.partial(attend_kernel, tiles),
        in_specs=[smem, smem, hbm, hbm, hbm],
        out_specs=pl.BlockSpec(memory_space=pltpu.VMEM),
        out_shape=jax.ShapeDtypeStruct((len(tiles), HB, TQ, HD), jnp.bfloat16),
        scratch_shapes=[
            pltpu.VMEM((len(tiles), HB, TQ, HD), jnp.bfloat16),
            pltpu.VMEM((NWIN, SHARD, HD), jnp.bfloat16),
            pltpu.VMEM((NWIN, SHARD, 2 * HD), jnp.bfloat16),
            pltpu.VMEM((HB, TQ, 2 * HD), jnp.float32),
            pltpu.VMEM((TQ, HD), jnp.float32),
            pltpu.VMEM((TQ, HD), jnp.float32),
            pltpu.SMEM((NWIN,), jnp.int32),
            pltpu.SemaphoreType.DMA((len(tiles),)),
            pltpu.SemaphoreType.DMA((2, NWIN)),
        ],
        compiler_params=pltpu.CompilerParams(vmem_limit_bytes=60 * 2**20),
        cost_estimate=pl.CostEstimate(flops=len(tiles) * 10**10, bytes_accessed=6 * 2**20, transcendentals=0),
        name="attend",
    )(doc_lengths, limits, q, qf, win)


def local(queries, keys, values, doc_lengths, tasks, w_out):
    n_tok = lax.axis_size("tok")
    n_head = lax.axis_size("head")
    t = lax.axis_index("tok")
    z = lax.axis_index("head")
    core = lax.rem(t, 2)
    width = w_out.shape[1] // n_head
    limits = tasks.reshape(-1, 8, 5)[:, 0, 2:4].reshape(-1)
    nx = 4
    qf, win = fetch(queries, keys, values, n_tok // (2 * nx), nx)
    swap = [(i, i ^ 1) for i in range(n_tok)]
    weights = w_out.reshape(2 * HB, HD, -1)
    rounds = {d: [(i, (i + d) % n_head) for i in range(n_head)] for d in range(1, n_head)}
    mine, theirs, sums = {}, {}, []
    for tiles in CALLS:
        out = attend(tiles, queries, qf, win, doc_lengths, limits)
        done = []
        for i, (side, r) in enumerate(tiles):
            if side:
                theirs[r] = lax.ppermute(out[i], "tok", swap)
            else:
                mine[r] = out[i]
                done.append(r)
        for r in done:
            lower = jnp.where(core == 0, mine[r], theirs[r])
            upper = jnp.where(core == 0, theirs[r], mine[r])
            part = jnp.einsum(
                "hte,hed->td",
                jnp.concatenate([lower, upper], axis=0),
                weights,
                preferred_element_type=jnp.float32,
            ).astype(jnp.bfloat16)
            total = lax.dynamic_slice_in_dim(part, z * width, width, 1).astype(jnp.float32)
            for d in range(1, n_head):
                block = lax.dynamic_slice_in_dim(part, lax.rem(z + d, n_head) * width, width, 1)
                got = lax.ppermute(block, "head", rounds[d])
                total = total + got.astype(jnp.float32)
            sums.append(total.astype(jnp.bfloat16))
    return jnp.concatenate(sums, axis=0)


def solution(mesh):
    in_specs = (
        P("head", "tok", None),
        P("head", "tok", None),
        P("head", "tok", None),
        P(),
        P(),
        P("head", None),
    )
    return jax.shard_map(local, mesh=mesh, in_specs=in_specs, out_specs=P("tok", "head"), check_vma=False)
```

```python
import functools
import math

import jax
import jax.numpy as jnp
from jax import lax
from jax.experimental import pallas as pl
from jax.experimental.pallas import tpu as pltpu
from jax.sharding import PartitionSpec as P

MESH = pl.DeviceIdType.MESH
SHARD = 1024
CHIP = 2 * SHARD
HD = 128
BACK = 4
WIN = (BACK + 1) * CHIP
TQ = 256
TILES = CHIP // TQ
HALF = SHARD // TQ
SMALL = 512
HB = 4
QBLK = 512
NDOC = 16
NBLK = CHIP // QBLK
C = math.log2(math.e) / math.sqrt(HD)
FLOOR = -1e30
BIG = 4096.0
NX = 4


def step_kernel(
    ny, nz, doc_ref, lim_ref, q_ref, k_ref, v_ref, w_ref, out_ref,
    kwin, vwin, kaug, qall, qs, acc, peak, wv, own_att, fsend, frecv, zsend, zrecv, psum, relay,
    load_sem, send_sem, recv_sem, fwd_sem, got_sem, swap_sem, back_send, back_recv, z_send, z_recv,
):
    t = lax.axis_index("tok")
    z = lax.axis_index("head")
    chip = t // 2
    k = lax.rem(t, 2)
    y = chip // NX
    x = lax.rem(chip, NX)

    def at(row, col):
        return (row * NX + col) * 2 + k

    partner = t + 1 - 2 * k
    down = at(lax.rem(y + 1, ny), x)
    up = at(lax.rem(y + ny - 1, ny), x)
    right = at(y, lax.rem(x + 1, NX))
    left = at(y, lax.rem(x + NX - 1, NX))
    depth = [lax.rem(z + d, nz) for d in range(nz)]
    bar = pltpu.get_barrier_semaphore()
    for p in (partner, down, up, right, left):
        pl.semaphore_signal(bar, inc=1, device_id={"tok": p}, device_id_type=MESH)
    for d in range(1, nz):
        pl.semaphore_signal(bar, inc=1, device_id={"head": depth[d]}, device_id_type=MESH)
    pl.semaphore_wait(bar, 5 + nz - 1)

    def remote(src, dst, s, r, tok):
        return pltpu.make_async_remote_copy(
            src_ref=src, dst_ref=dst, send_sem=s, recv_sem=r, device_id={"tok": tok}, device_id_type=MESH
        )

    mine = (k_ref.at[0], v_ref.at[0])
    wins = (kwin, vwin)

    def slot(d, m):
        row = (BACK - d) * CHIP + k * SHARD
        return wins[m].at[pl.ds(pl.multiple_of(row, SHARD), SHARD)]

    swaps = [remote(mine[m], slot(0, m), fwd_sem.at[0, m], got_sem.at[0, m], partner) for m in range(2)]
    for cp in swaps:
        cp.start()
    here = pl.ds(pl.multiple_of(k * SHARD, SHARD), SHARD)
    qswap = remote(q_ref.at[pl.ds((1 - k) * HB, HB)], qall.at[:, here], swap_sem.at[0], swap_sem.at[1], partner)
    qswap.start()
    above = [remote(mine[m], slot(BACK, m), send_sem.at[BACK, m], recv_sem.at[BACK, m], down) for m in range(2)]
    for cp in above:
        cp.start()

    def across(d, m, src):
        if d == 2:
            return remote(src, relay.at[m], send_sem.at[2, m], recv_sem.at[0, m], right if m == 0 else left)
        return remote(src, slot(d, m), send_sem.at[d, m], recv_sem.at[d, m], right if d == 1 else left)

    order = (1, 3, 2)
    for m in range(2):
        for d in order:

            @pl.when(x + d < NX)
            def _():
                across(d, m, mine[m]).start()

    loads = [pltpu.make_async_copy(mine[m], slot(0, m), load_sem.at[m]) for m in range(2)]
    loads.append(pltpu.make_async_copy(q_ref.at[pl.ds(k * HB, HB)], qall.at[:, here], load_sem.at[2]))
    wload = pltpu.make_async_copy(w_ref, wv, load_sem.at[3])
    for cp in loads:
        cp.start()
    wload.start()

    onward = []

    def pass_on(d, m):
        cp = remote(slot(d, m), slot(d, m), fwd_sem.at[d, m], got_sem.at[d, m], partner)
        cp.start()
        onward.append(cp)

    base = (chip - BACK) * CHIP
    lane = lax.broadcasted_iota(jnp.int32, (8, HD), 1)
    lo = jnp.zeros((8, HD), jnp.int32)
    hi = jnp.zeros((8, HD), jnp.int32)
    start = -base
    for d in range(NDOC):
        lo = jnp.where(lane == d, start, lo)
        start = start + doc_ref[d]
        hi = jnp.where(lane == d, start, hi)
    for b in range(NBLK):
        blk = chip * NBLK + b
        lo = jnp.where(lane == NDOC + b, lim_ref[2 * blk] * QBLK - base, lo)
        hi = jnp.where(lane == NDOC + b, lim_ref[2 * blk + 1] * QBLK - base, hi)

    def marks(row0, rows):
        pos = row0 + lax.broadcasted_iota(jnp.int32, (rows, HD), 0)
        col = lax.broadcasted_iota(jnp.int32, (rows, HD), 1)
        inside = (pos >= lo[:1]) & (pos < hi[:1])
        return pos, col, inside

    def key_marks(i, _):
        row0 = pl.multiple_of(i * TQ, TQ)
        _, col, inside = marks(row0, TQ)
        limit = (col >= NDOC) & (col < NDOC + NBLK)
        seen = jnp.where(inside, 1.0, 0.0)
        kaug[pl.ds(row0, TQ), :] = jnp.where(limit, 1.0 - seen, jnp.where(col < NDOC, seen, 0.0)).astype(jnp.bfloat16)
        return 0

    lax.fori_loop(0, WIN // TQ, key_marks, 0)

    for cp in loads:
        cp.wait()
    for cp in swaps:
        cp.wait_recv()
    qswap.wait_recv()

    def query_marks(g, _):
        row0 = pl.multiple_of(g * TQ, TQ)
        pos, col, inside = marks(BACK * CHIP + row0, TQ)
        block = (pos - BACK * CHIP) // QBLK
        hide = jnp.where(col < NDOC, jnp.where(inside, 0.0, -BIG), jnp.where(col == NDOC + block, -BIG, 0.0))
        hide = hide.astype(jnp.bfloat16)
        for h in range(HB):
            qs[g, h, :, pl.ds(HD, HD)] = hide
            qs[g, h, :, pl.ds(0, HD)] = (qall[h, pl.ds(row0, TQ), :].astype(jnp.float32) * C).astype(jnp.bfloat16)
        return 0

    lax.fori_loop(0, TILES, query_marks, 0)

    def attend(g, row, width, first):
        row = pl.multiple_of(row, TQ)
        kb = jnp.concatenate([kwin[pl.ds(row, width), :], kaug[pl.ds(row, width), :]], axis=1)
        vb = jnp.concatenate([vwin[pl.ds(row, width), :], jnp.ones((width, HD), jnp.bfloat16)], axis=1)
        if first:
            gap = BACK * CHIP + g * TQ - row
            rows = lax.broadcasted_iota(jnp.int32, (TQ, width), 0)
            cols = lax.broadcasted_iota(jnp.int32, (TQ, width), 1)
            ahead = cols > rows + gap
        for h in range(HB):
            s = lax.dot_general(qs[g, h], kb, (((1,), (1,)), ((), ())), preferred_element_type=jnp.float32)
            if first:
                s = jnp.where(ahead, FLOOR, s)
            groups = [s[:, i * HD : (i + 1) * HD] for i in range(width // HD)]
            top = functools.reduce(jnp.maximum, groups)
            top = jnp.max(top, axis=1, keepdims=True)
            if first:
                new = jnp.broadcast_to(top, (TQ, HD))
            else:
                old = peak[g, h]
                new = jnp.maximum(old, top)
            p = jnp.concatenate([jnp.exp2(s_i - new).astype(jnp.bfloat16) for s_i in groups], axis=1)
            add = jnp.dot(p, vb, preferred_element_type=jnp.float32)
            peak[g, h] = new
            if first:
                acc[g, h] = add
            else:
                keep = jnp.exp2(old - new)
                acc[g, h] = acc[g, h] * jnp.concatenate([keep, keep], axis=1) + add

    per = SMALL // TQ

    def own_chip(g, _):
        edge = BACK * CHIP + g // per * SMALL
        attend(g, edge, SMALL, True)

        def before(i, _):
            attend(g, BACK * CHIP + i * SMALL, SMALL, False)
            return 0

        lax.fori_loop(0, g // per, before, 0)
        return 0

    def far_chip(g, _):
        def after(i, _):
            attend(g, i * SMALL, SMALL, False)
            return 0

        lax.fori_loop(g // per, CHIP // SMALL, after, 0)
        return 0

    def next_chip(g, _):
        attend(g, (BACK - 1) * CHIP, CHIP, False)
        return 0

    for m in range(2):
        lax.fori_loop(4 * m, 4 * m + 4, own_chip, 0)
        above[m].wait_recv()
        for d in order:

            @pl.when(x + d >= NX)
            def _():
                across(d, m, slot(BACK, m)).start()

        pass_on(BACK, m)

    hops = []
    for m in range(2):
        across(2, m, mine[m]).wait_recv()
        hop = remote(relay.at[m], slot(2, m), send_sem.at[0, m], recv_sem.at[2, m], right if m == 0 else left)
        hop.start()
        hops.append(hop)
    for m in range(2):
        onward[m].wait_recv()
    lax.fori_loop(0, 4, far_chip, 0)
    for d in (1, 3):
        for m in range(2):
            across(d, m, mine[m]).wait_recv()
            pass_on(d, m)
    lax.fori_loop(4, TILES, far_chip, 0)
    for m in range(2):
        hops[m].wait_recv()
        pass_on(2, m)
    for m in range(2):
        onward[2 + m].wait_recv()
    lax.fori_loop(0, TILES, next_chip, 0)
    for cp in onward[4:]:
        cp.wait_recv()
    wload.wait()

    def back_copy(n):
        return remote(fsend.at[n], frecv.at[n], back_send.at[n], back_recv.at[n], partner)

    def head_copy(n, d):
        return pltpu.make_async_remote_copy(
            src_ref=zsend.at[n, d - 1],
            dst_ref=zrecv.at[n, d - 1],
            send_sem=z_send.at[n, d - 1],
            recv_sem=z_recv.at[n, d - 1],
            device_id={"head": depth[d]},
            device_id_type=MESH,
        )

    width = out_ref.shape[1]

    def finish(n):
        total = psum[n]
        for d in range(1, nz):
            head_copy(n, d).wait_recv()
            total = total + zrecv[n, d - 1].astype(jnp.float32)
        out_ref[pl.ds(pl.multiple_of(n * TQ, TQ), TQ), :] = total.astype(out_ref.dtype)

    def complete(i, _):
        foreign = (i == 0) | (i == 1) | (i == 3) | (i == 5)
        n = jnp.where(foreign, (i + 1) // 2, jnp.where(i == 7, 3, i // 2 - 1))
        g = jnp.where(foreign, 1 - k, k) * HALF + n

        def chips(c, _):
            attend(g, (1 + c) * CHIP, CHIP, False)
            return 0

        lax.fori_loop(0, 2, chips, 0)
        attended = []
        for h in range(HB):
            both = acc[g, h]
            attended.append((both[:, :HD] / both[:, HD:]).astype(jnp.bfloat16))
        attended = jnp.concatenate(attended, axis=1)

        @pl.when(foreign)
        def _():
            fsend[n] = attended
            back_copy(n).start()

        @pl.when(jnp.logical_not(foreign))
        def _():
            own_att[...] = attended
            back_copy(n).wait_recv()
            near = pl.ds(pl.multiple_of(k * (HB * HD), HB * HD), HB * HD)
            away = pl.ds(pl.multiple_of((1 - k) * (HB * HD), HB * HD), HB * HD)
            for d in (2, 1, 3, 0):
                cols = pl.ds(pl.multiple_of(depth[d] * width, width), width)
                part = jnp.dot(own_att[...], wv[near, cols], preferred_element_type=jnp.float32)
                part = part + jnp.dot(frecv[n], wv[away, cols], preferred_element_type=jnp.float32)
                if d:
                    zsend[n, d - 1] = part.astype(jnp.bfloat16)
                    head_copy(n, d).start()
                else:
                    psum[n] = part.astype(jnp.bfloat16).astype(jnp.float32)

            @pl.when(n > 0)
            def _():
                finish(n - 1)

        return 0

    lax.fori_loop(0, TILES, complete, 0)
    finish(HALF - 1)

    for m in range(2):
        swaps[m].wait_send()
        above[m].wait_send()
        hops[m].wait_send()
        for d in order:
            across(d, m, mine[m]).wait_send()
    qswap.wait_send()
    for cp in onward:
        cp.wait_send()
    for n in range(HALF):
        back_copy(n).wait_send()
        for d in range(1, nz):
            head_copy(n, d).wait_send()


def local(queries, keys, values, doc_lengths, tasks, w_out):
    ny = lax.axis_size("tok") // (2 * NX)
    nz = lax.axis_size("head")
    width = w_out.shape[1] // nz
    limits = tasks.reshape(-1, 8, 5)[:, 0, 2:4].reshape(-1)
    smem = pl.BlockSpec(memory_space=pltpu.SMEM)
    hbm = pl.BlockSpec(memory_space=pl.ANY)
    bf16, f32 = jnp.bfloat16, jnp.float32
    dma = pltpu.SemaphoreType.DMA
    return pl.pallas_call(
        functools.partial(step_kernel, ny, nz),
        in_specs=[smem, smem, hbm, hbm, hbm, hbm],
        out_specs=pl.BlockSpec(memory_space=pltpu.VMEM),
        out_shape=jax.ShapeDtypeStruct((SHARD, width), bf16),
        scratch_shapes=[
            pltpu.VMEM((WIN, HD), bf16),
            pltpu.VMEM((WIN, HD), bf16),
            pltpu.VMEM((WIN, HD), bf16),
            pltpu.VMEM((HB, CHIP, HD), bf16),
            pltpu.VMEM((TILES, HB, TQ, 2 * HD), bf16),
            pltpu.VMEM((TILES, HB, TQ, 2 * HD), f32),
            pltpu.VMEM((TILES, HB, TQ, HD), f32),
            pltpu.VMEM(w_out.shape, bf16),
            pltpu.VMEM((TQ, HB * HD), bf16),
            pltpu.VMEM((HALF, TQ, HB * HD), bf16),
            pltpu.VMEM((HALF, TQ, HB * HD), bf16),
            pltpu.VMEM((HALF, nz - 1, TQ, width), bf16),
            pltpu.VMEM((HALF, nz - 1, TQ, width), bf16),
            pltpu.VMEM((HALF, TQ, width), f32),
            pltpu.VMEM((2, SHARD, HD), bf16),
            dma((4,)),
            dma((BACK + 1, 2)),
            dma((BACK + 1, 2)),
            dma((BACK + 1, 2)),
            dma((BACK + 1, 2)),
            dma((2,)),
            dma((HALF,)),
            dma((HALF,)),
            dma((HALF, nz - 1)),
            dma((HALF, nz - 1)),
        ],
        compiler_params=pltpu.CompilerParams(
            collective_id=0, has_side_effects=True, vmem_limit_bytes=67043328
        ),
        name="attention",
    )(doc_lengths, limits, queries, keys, values, w_out)


def solution(mesh):
    in_specs = (
        P("head", "tok", None),
        P("head", "tok", None),
        P("head", "tok", None),
        P(),
        P(),
        P("head", None),
    )
    return jax.shard_map(local, mesh=mesh, in_specs=in_specs, out_specs=P("tok", "head"), check_vma=False)
```

```python
import functools
import math

import jax
import jax.numpy as jnp
from jax import lax
from jax.experimental import pallas as pl
from jax.experimental.pallas import tpu as pltpu
from jax.sharding import PartitionSpec as P

MESH = pl.DeviceIdType.MESH
SHARD = 1024
CHIP = 2 * SHARD
HD = 128
BACK = 4
WIN = (BACK + 1) * CHIP
TQ = 256
TILES = CHIP // TQ
HALF = SHARD // TQ
SMALL = 512
NEXT = 256
HB = 4
QBLK = 512
NDOC = 16
NBLK = CHIP // QBLK
C = math.log2(math.e) / math.sqrt(HD)
FLOOR = -1e30
BIG = 4096.0
NX = 4
GROUP = 8
ROWS = NBLK * GROUP
SAFE = 90.0


def step_kernel(
    ny, nz, running, doc_ref, task_ref, q_ref, k_ref, v_ref, w_ref, out_ref, norm_ref,
    kwin, vwin, kaug, qall, qs, acc, peak, wv, own_att, fsend, frecv, zsend, zrecv, psum, relay, task,
    nsend, nrecv,
    load_sem, send_sem, recv_sem, fwd_sem, got_sem, swap_sem, back_send, back_recv, z_send, z_recv, n_send, n_recv,
):
    t = lax.axis_index("tok")
    z = lax.axis_index("head")
    chip = t // 2
    k = lax.rem(t, 2)
    y = chip // NX
    x = lax.rem(chip, NX)

    def at(row, col):
        return (row * NX + col) * 2 + k

    partner = t + 1 - 2 * k
    down = at(lax.rem(y + 1, ny), x)
    up = at(lax.rem(y + ny - 1, ny), x)
    right = at(y, lax.rem(x + 1, NX))
    left = at(y, lax.rem(x + NX - 1, NX))
    depth = [lax.rem(z + d, nz) for d in range(nz)]
    bar = pltpu.get_barrier_semaphore()
    around = [
        [{"head": depth[d]} for d in range(1, nz)],
        [{"tok": at(y, lax.rem(x + d, NX))} for d in range(1, NX)],
        [{"tok": at(lax.rem(y + d, ny), x)} for d in range(1, ny)],
        [{"tok": partner}],
    ]
    peers = [p for group in around for p in group]
    for p in peers:
        pl.semaphore_signal(bar, inc=1, device_id=p, device_id_type=MESH)
    pl.semaphore_wait(bar, len(peers))

    def remote(src, dst, s, r, tok):
        return pltpu.make_async_remote_copy(
            src_ref=src, dst_ref=dst, send_sem=s, recv_sem=r, device_id={"tok": tok}, device_id_type=MESH
        )

    mine = (k_ref.at[0], v_ref.at[0])
    wins = (kwin, vwin)

    def slot(d, m):
        row = (BACK - d) * CHIP + k * SHARD
        return wins[m].at[pl.ds(pl.multiple_of(row, SHARD), SHARD)]

    swaps = [remote(mine[m], slot(0, m), fwd_sem.at[0, m], got_sem.at[0, m], partner) for m in range(2)]
    for cp in swaps:
        cp.start()
    here = pl.ds(pl.multiple_of(k * SHARD, SHARD), SHARD)
    qswap = remote(q_ref.at[pl.ds((1 - k) * HB, HB)], qall.at[:, here], swap_sem.at[0], swap_sem.at[1], partner)
    qswap.start()
    above = [remote(mine[m], slot(BACK, m), send_sem.at[BACK, m], recv_sem.at[BACK, m], down) for m in range(2)]
    for cp in above:
        cp.start()

    def across(d, m, src):
        if d == 2:
            return remote(src, relay.at[m], send_sem.at[2, m], recv_sem.at[0, m], right if m == 0 else left)
        return remote(src, slot(d, m), send_sem.at[d, m], recv_sem.at[d, m], right if d == 1 else left)

    order = (1, 3, 2)
    for m in range(2):
        for d in order:

            @pl.when(x + d < NX)
            def _():
                across(d, m, mine[m]).start()

    loads = [pltpu.make_async_copy(mine[m], slot(0, m), load_sem.at[m]) for m in range(2)]
    loads.append(pltpu.make_async_copy(q_ref.at[pl.ds(k * HB, HB)], qall.at[:, here], load_sem.at[2]))
    loads.append(pltpu.make_async_copy(task_ref.at[pl.ds(pl.multiple_of(chip * ROWS, ROWS), ROWS)], task, load_sem.at[4]))
    wload = pltpu.make_async_copy(w_ref, wv, load_sem.at[3])
    for cp in loads:
        cp.start()
    wload.start()
    loads[3].wait()

    onward = []

    def pass_on(d, m):
        cp = remote(slot(d, m), slot(d, m), fwd_sem.at[d, m], got_sem.at[d, m], partner)
        cp.start()
        onward.append(cp)

    base = (chip - BACK) * CHIP
    lane = lax.broadcasted_iota(jnp.int32, (8, HD), 1)
    lo = jnp.zeros((8, HD), jnp.int32)
    hi = jnp.zeros((8, HD), jnp.int32)
    start = -base
    for d in range(NDOC):
        lo = jnp.where(lane == d, start, lo)
        start = start + doc_ref[d]
        hi = jnp.where(lane == d, start, hi)
    for b in range(NBLK):
        lo = jnp.where(lane == NDOC + b, task[b * GROUP, 2] * QBLK - base, lo)
        hi = jnp.where(lane == NDOC + b, task[b * GROUP, 3] * QBLK - base, hi)

    def marks(row0, rows):
        pos = row0 + lax.broadcasted_iota(jnp.int32, (rows, HD), 0)
        col = lax.broadcasted_iota(jnp.int32, (rows, HD), 1)
        inside = (pos >= lo[:1]) & (pos < hi[:1])
        return pos, col, inside

    def key_marks(i, _):
        row0 = pl.multiple_of(i * TQ, TQ)
        _, col, inside = marks(row0, TQ)
        limit = (col >= NDOC) & (col < NDOC + NBLK)
        seen = jnp.where(inside, 1.0, 0.0)
        kaug[pl.ds(row0, TQ), :] = jnp.where(limit, 1.0 - seen, jnp.where(col < NDOC, seen, 0.0)).astype(jnp.bfloat16)
        return 0

    lax.fori_loop(0, WIN // TQ, key_marks, 0)

    for cp in loads[:3]:
        cp.wait()
    for cp in swaps:
        cp.wait_recv()
    qswap.wait_recv()

    def query_marks(g, most):
        row0 = pl.multiple_of(g * TQ, TQ)
        pos, col, inside = marks(BACK * CHIP + row0, TQ)
        block = (pos - BACK * CHIP) // QBLK
        hide = jnp.where(col < NDOC, jnp.where(inside, 0.0, -BIG), jnp.where(col == NDOC + block, -BIG, 0.0))
        hide = hide.astype(jnp.bfloat16)
        for h in range(HB):
            qs[h, pl.ds(row0, TQ), pl.ds(HD, HD)] = hide
            scaled = (qall[h, pl.ds(row0, TQ), :].astype(jnp.float32) * C).astype(jnp.bfloat16)
            qs[h, pl.ds(row0, TQ), pl.ds(0, HD)] = scaled
            if not running:
                most = jnp.maximum(most, squares(scaled))
        return most

    def squares(rows):
        return jnp.dot(rows * rows, jnp.ones((HD, HD), jnp.bfloat16), preferred_element_type=jnp.float32)

    most = lax.fori_loop(0, TILES, query_marks, jnp.zeros((TQ, HD), jnp.float32))

    def norm_copies(phase):
        return [
            pltpu.make_async_remote_copy(
                src_ref=nsend.at[phase],
                dst_ref=nrecv.at[phase, i],
                send_sem=n_send.at[phase, i],
                recv_sem=n_recv.at[phase, i],
                device_id=p,
                device_id_type=MESH,
            )
            for i, p in enumerate(around[phase])
        ]

    def spread(phase, norms):
        if running:
            return None
        if phase:
            for i, cp in enumerate(norm_copies(phase - 1)):
                cp.wait_recv()
                norms = jnp.maximum(norms, nrecv[phase - 1, i])
        if phase < len(around):
            nsend[phase] = norms
            for cp in norm_copies(phase):
                cp.start()
        else:
            norm_ref[...] = norms
        return norms

    norms = None
    if not running:
        most_q = jnp.max(most, axis=0, keepdims=True)
        most_k = jnp.max(squares(kwin[pl.ds(pl.multiple_of(BACK * CHIP + k * SHARD, SHARD), SHARD), :]), axis=0, keepdims=True)
        row = lax.broadcasted_iota(jnp.int32, (16, HD), 0)
        norms = jnp.where(row < 8, jnp.broadcast_to(most_q, (16, HD)), jnp.broadcast_to(most_k, (16, HD)))
    norms = spread(0, norms)

    def attend(tile, size, row, width, first):
        tile = pl.multiple_of(tile, TQ)
        row = pl.multiple_of(row, TQ)
        here = pl.ds(tile, size)
        kb = jnp.concatenate([kwin[pl.ds(row, width), :], kaug[pl.ds(row, width), :]], axis=1)
        vb = jnp.concatenate([vwin[pl.ds(row, width), :], jnp.ones((width, HD), jnp.bfloat16)], axis=1)
        if first:
            rows = lax.broadcasted_iota(jnp.int32, (size, width), 0)
            cols = lax.broadcasted_iota(jnp.int32, (size, width), 1)
            ahead = cols > rows
        for h in range(HB):
            s = lax.dot_general(qs[h, here, :], kb, (((1,), (1,)), ((), ())), preferred_element_type=jnp.float32)
            if first:
                s = jnp.where(ahead, FLOOR, s)
            if not running:
                add = jnp.dot(jnp.exp2(s).astype(jnp.bfloat16), vb, preferred_element_type=jnp.float32)
                acc[h, here, :] = add if first else acc[h, here, :] + add
                continue
            groups = [s[:, i * HD : (i + 1) * HD] for i in range(width // HD)]
            top = functools.reduce(jnp.maximum, groups)
            top = jnp.max(top, axis=1, keepdims=True)
            if first:
                new = jnp.broadcast_to(top, (size, HD))
            else:
                old = peak[h, here, :]
                new = jnp.maximum(old, top)
            p = jnp.concatenate([jnp.exp2(s_i - new).astype(jnp.bfloat16) for s_i in groups], axis=1)
            add = jnp.dot(p, vb, preferred_element_type=jnp.float32)
            peak[h, here, :] = new
            if first:
                acc[h, here, :] = add
            else:
                keep = jnp.exp2(old - new)
                acc[h, here, :] = acc[h, here, :] * jnp.concatenate([keep, keep], axis=1) + add

    def own_chip(j, _):
        attend(j * SMALL, SMALL, BACK * CHIP + j * SMALL, SMALL, True)

        def before(i, _):
            attend(j * SMALL, SMALL, BACK * CHIP + i * SMALL, SMALL, False)
            return 0

        lax.fori_loop(0, j, before, 0)
        return 0

    def far_chip(j, _):
        def after(i, _):
            attend(j * SMALL, SMALL, i * SMALL, SMALL, False)
            return 0

        lax.fori_loop(j, CHIP // SMALL, after, 0)
        return 0

    def next_chip(j, _):
        attend(j * NEXT, NEXT, (BACK - 1) * CHIP, CHIP, False)
        return 0

    for m in range(2):
        lax.fori_loop(2 * m, 2 * m + 2, own_chip, 0)
        above[m].wait_recv()
        for d in order:

            @pl.when(x + d >= NX)
            def _():
                across(d, m, slot(BACK, m)).start()

        pass_on(BACK, m)
        norms = spread(1 + m, norms)

    hops = []
    for m in range(2):
        across(2, m, mine[m]).wait_recv()
        hop = remote(relay.at[m], slot(2, m), send_sem.at[0, m], recv_sem.at[2, m], right if m == 0 else left)
        hop.start()
        hops.append(hop)
    for m in range(2):
        onward[m].wait_recv()
    lax.fori_loop(0, 1, far_chip, 0)
    norms = spread(3, norms)
    for d in (1, 3):
        for m in range(2):
            across(d, m, mine[m]).wait_recv()
            pass_on(d, m)
    lax.fori_loop(1, CHIP // SMALL, far_chip, 0)
    norms = spread(4, norms)
    for m in range(2):
        hops[m].wait_recv()
        pass_on(2, m)
    for m in range(2):
        onward[2 + m].wait_recv()
    lax.fori_loop(0, CHIP // NEXT, next_chip, 0)
    for cp in onward[4:]:
        cp.wait_recv()
    wload.wait()

    def back_copy(n):
        return remote(fsend.at[n], frecv.at[n], back_send.at[n], back_recv.at[n], partner)

    def head_copy(n, d):
        return pltpu.make_async_remote_copy(
            src_ref=zsend.at[n, d - 1],
            dst_ref=zrecv.at[n, d - 1],
            send_sem=z_send.at[n, d - 1],
            recv_sem=z_recv.at[n, d - 1],
            device_id={"head": depth[d]},
            device_id_type=MESH,
        )

    width = out_ref.shape[1]

    def finish(n):
        total = psum[n]
        for d in range(1, nz):
            head_copy(n, d).wait_recv()
            total = total + zrecv[n, d - 1].astype(jnp.float32)
        out_ref[pl.ds(pl.multiple_of(n * TQ, TQ), TQ), :] = total.astype(out_ref.dtype)

    def complete(i, _):
        foreign = (i == 0) | (i == 1) | (i == 3) | (i == 5)
        n = jnp.where(foreign, (i + 1) // 2, jnp.where(i == 7, 3, i // 2 - 1))
        tile = pl.multiple_of((jnp.where(foreign, 1 - k, k) * HALF + n) * TQ, TQ)

        def chips(c, _):
            attend(tile, TQ, (1 + c) * CHIP, CHIP, False)
            return 0

        lax.fori_loop(0, 2, chips, 0)
        attended = []
        for h in range(HB):
            both = acc[h, pl.ds(tile, TQ), :]
            attended.append((both[:, :HD] / both[:, HD:]).astype(jnp.bfloat16))
        attended = jnp.concatenate(attended, axis=1)

        @pl.when(foreign)
        def _():
            fsend[n] = attended
            back_copy(n).start()

        @pl.when(jnp.logical_not(foreign))
        def _():
            own_att[...] = attended
            back_copy(n).wait_recv()
            near = pl.ds(pl.multiple_of(k * (HB * HD), HB * HD), HB * HD)
            away = pl.ds(pl.multiple_of((1 - k) * (HB * HD), HB * HD), HB * HD)
            for d in (2, 1, 3, 0):
                cols = pl.ds(pl.multiple_of(depth[d] * width, width), width)
                part = jnp.dot(own_att[...], wv[near, cols], preferred_element_type=jnp.float32)
                part = part + jnp.dot(frecv[n], wv[away, cols], preferred_element_type=jnp.float32)
                if d:
                    zsend[n, d - 1] = part.astype(jnp.bfloat16)
                    head_copy(n, d).start()
                else:
                    psum[n] = part.astype(jnp.bfloat16).astype(jnp.float32)

            @pl.when(n > 0)
            def _():
                finish(n - 1)

        return 0

    lax.fori_loop(0, TILES, complete, 0)
    finish(HALF - 1)

    for m in range(2):
        swaps[m].wait_send()
        above[m].wait_send()
        hops[m].wait_send()
        for d in order:
            across(d, m, mine[m]).wait_send()
    qswap.wait_send()
    for cp in onward:
        cp.wait_send()
    if running:
        norm_ref[...] = jnp.zeros(norm_ref.shape, jnp.float32)
    else:
        for phase in range(len(around)):
            for cp in norm_copies(phase):
                cp.wait_send()
    for n in range(HALF):
        back_copy(n).wait_send()
        for d in range(1, nz):
            head_copy(n, d).wait_send()


def step(running, ny, nz, args):
    doc_lengths, tasks, queries, keys, values, w_out = args
    width = w_out.shape[1] // nz
    smem = pl.BlockSpec(memory_space=pltpu.SMEM)
    hbm = pl.BlockSpec(memory_space=pl.ANY)
    vmem = pl.BlockSpec(memory_space=pltpu.VMEM)
    bf16, f32 = jnp.bfloat16, jnp.float32
    dma = pltpu.SemaphoreType.DMA
    few = 1 if running else 4
    return pl.pallas_call(
        functools.partial(step_kernel, ny, nz, running),
        in_specs=[smem, hbm, hbm, hbm, hbm, hbm],
        out_specs=[vmem, vmem],
        out_shape=[jax.ShapeDtypeStruct((SHARD, width), bf16), jax.ShapeDtypeStruct((16, HD), f32)],
        scratch_shapes=[
            pltpu.VMEM((WIN, HD), bf16),
            pltpu.VMEM((WIN, HD), bf16),
            pltpu.VMEM((WIN, HD), bf16),
            pltpu.VMEM((HB, CHIP, HD), bf16),
            pltpu.VMEM((HB, CHIP, 2 * HD), bf16),
            pltpu.VMEM((HB, CHIP, 2 * HD), f32),
            pltpu.VMEM((HB if running else 1, CHIP, HD), f32),
            pltpu.VMEM(w_out.shape, bf16),
            pltpu.VMEM((TQ, HB * HD), bf16),
            pltpu.VMEM((HALF, TQ, HB * HD), bf16),
            pltpu.VMEM((HALF, TQ, HB * HD), bf16),
            pltpu.VMEM((HALF, nz - 1, TQ, width), bf16),
            pltpu.VMEM((HALF, nz - 1, TQ, width), bf16),
            pltpu.VMEM((HALF, TQ, width), f32),
            pltpu.VMEM((2, SHARD, HD), bf16),
            pltpu.SMEM((ROWS, tasks.shape[1]), jnp.int32),
            pltpu.VMEM((few, 16, HD), f32),
            pltpu.VMEM((few, 3, 16, HD), f32),
            dma((5,)),
            dma((BACK + 1, 2)),
            dma((BACK + 1, 2)),
            dma((BACK + 1, 2)),
            dma((BACK + 1, 2)),
            dma((2,)),
            dma((HALF,)),
            dma((HALF,)),
            dma((HALF, nz - 1)),
            dma((HALF, nz - 1)),
            dma((few, 3)),
            dma((few, 3)),
        ],
        compiler_params=pltpu.CompilerParams(
            collective_id=int(running), has_side_effects=True, vmem_limit_bytes=67043328
        ),
        name="running" if running else "plain",
    )(doc_lengths, tasks, queries, keys, values, w_out)


def local(queries, keys, values, doc_lengths, tasks, w_out):
    ny = lax.axis_size("tok") // (2 * NX)
    nz = lax.axis_size("head")
    args = (doc_lengths, tasks, queries, keys, values, w_out)
    out, norms = step(False, ny, nz, args)
    safe = norms[0, 0] * norms[8, 0] <= SAFE * SAFE
    return lax.cond(safe, lambda: out, lambda: step(True, ny, nz, args)[0])


def solution(mesh):
    in_specs = (
        P("head", "tok", None),
        P("head", "tok", None),
        P("head", "tok", None),
        P(),
        P(),
        P("head", None),
    )
    return jax.shard_map(local, mesh=mesh, in_specs=in_specs, out_specs=P("tok", "head"), check_vma=False)
```
